256 devices in a mesh: aln: 8 (over x, core), seq: 32 (over z, y).
Axes of the slice: x: 4, y: 4, z: 8, core: 2. Of those that a mesh axis runs over, the one named last changes fastest.
Arguments:
- embedded_homologs: bfloat16 [2048, 128, 768], P(('aln', 'seq')), parts along dimension 0, may hold values from -6 to 6
- homolog_tallies: int32 [8], P('aln'), parts along dimension 0, may hold values from 64 to 256
- horizontal_probe_matrix: bfloat16 [768, 768], replicated
- horizontal_lookup_matrix: bfloat16 [768, 768], replicated
- horizontal_content_matrix: bfloat16 [768, 768], replicated, may hold values from -0.21875 to 0.21875
- vertical_probe_matrix: bfloat16 [768, 768], replicated
- vertical_lookup_matrix: bfloat16 [768, 768], replicated
- vertical_content_matrix: bfloat16 [768, 768], replicated, may hold values from -0.21875 to 0.21875
Outputs:
- row_output: bfloat16 [2048, 128, 768], P(('aln', 'seq')), parts along dimension 0
- column_output: bfloat16 [2048, 128, 768], P(('aln', 'seq')), parts along dimension 0
The draws below stay inside these ranges and needn't reach their ends.
There are 8 independent parts, one for each index of `aln`. The reference program is written for one: setup_inputs(seed, part) draws one part's arguments, and reference() takes and returns one part's arrays. A program takes and returns all parts, laid end to end along the dimension named above; an argument that names none is the same for every part. Nothing has to cross between parts.
Inputs may be any that keep to these rules, and one draw needn't show every extreme that they name: Sequence slots from homolog_tallies[0] on are padding.
All inputs are finite; a program needn't handle non-finite values.
Results may differ from the reference program's by a relative error of at most 0.024.
Values may be sent and summed in bfloat16 or wider, within the bound.
No kernel may reach another device: no remote copies, remote signals or barrier semaphores. Data moves between devices by JAX's collectives and lax.ppermute only.
A program may use at most 128 MiB of HBM per device.

```python
import jax
import jax.numpy as jnp
from jax import lax

EMBED_DIMENSION = 768
H = 12
DH = 64
POSITION_TOTAL = 128
HOMOLOG_CAPACITY = 256


def paired_weights(key, salt):
    base = jax.random.fold_in(key, salt)
    first = jax.random.normal(jax.random.fold_in(base, 1), (EMBED_DIMENSION, EMBED_DIMENSION), jnp.float32) / jnp.sqrt(jnp.float32(EMBED_DIMENSION))
    other = jax.random.normal(jax.random.fold_in(base, 2), (EMBED_DIMENSION, EMBED_DIMENSION), jnp.float32) / jnp.sqrt(jnp.float32(EMBED_DIMENSION))
    second = other
    return (first, second)


def draw_horizontal_probe_matrix(key, part):
    return paired_weights(key, 11)[0].astype(jnp.bfloat16)


def draw_horizontal_lookup_matrix(key, part):
    return paired_weights(key, 11)[1].astype(jnp.bfloat16)


def draw_vertical_probe_matrix(key, part):
    return paired_weights(key, 23)[0].astype(jnp.bfloat16)


def draw_vertical_lookup_matrix(key, part):
    return paired_weights(key, 23)[1].astype(jnp.bfloat16)


def block_levels(rng, extent, shards, least, largest):
    loudness = 1.0
    for axis_at, parts in shards:
        draws = jax.random.uniform(jax.random.fold_in(jax.random.fold_in(rng, 6), axis_at), (parts,), jnp.float32, least / len(shards), largest / len(shards))
        loudness = loudness * jnp.repeat(jnp.exp(draws), extent[axis_at] // parts).reshape((-1,) + (1,) * (len(extent) - 1 - axis_at))
    return loudness


def gaussian(stream_key, dims, width, reach, split=(), kind=jnp.bfloat16):
    level = block_levels(stream_key, dims, split, -0.22, 0.18) if split else 1.0
    values = jax.random.normal(stream_key, dims, jnp.float32) * width * level
    return jnp.minimum(jnp.maximum(values, -reach), reach).astype(kind)


def setup_inputs(seed: int = 0, part: int = 0) -> dict:
    streams_of = jax.random.split(jax.random.key(seed), 9)
    part_keys = jax.random.split(jax.random.fold_in(streams_of[8], part), 9)
    return {
        "embedded_homologs": gaussian(part_keys[0], (HOMOLOG_CAPACITY, POSITION_TOTAL, EMBED_DIMENSION), 1.0, 6.0, ((0, 32),)),
        "homolog_tallies": jax.random.randint(part_keys[1], (1,), HOMOLOG_CAPACITY // 4, HOMOLOG_CAPACITY + 1).astype(jnp.int32),
        "horizontal_probe_matrix": draw_horizontal_probe_matrix(jax.random.fold_in(streams_of[8], 71), part),
        "horizontal_lookup_matrix": draw_horizontal_lookup_matrix(jax.random.fold_in(streams_of[8], 71), part),
        "horizontal_content_matrix": gaussian(streams_of[4], (EMBED_DIMENSION, EMBED_DIMENSION), EMBED_DIMENSION ** -0.5, 0.21875),
        "vertical_probe_matrix": draw_vertical_probe_matrix(jax.random.fold_in(streams_of[8], 71), part),
        "vertical_lookup_matrix": draw_vertical_lookup_matrix(jax.random.fold_in(streams_of[8], 71), part),
        "vertical_content_matrix": gaussian(streams_of[7], (EMBED_DIMENSION, EMBED_DIMENSION), EMBED_DIMENSION ** -0.5, 0.21875),
    }


def standardize_features(values):
    centre = lax.optimization_barrier(jnp.mean(values, axis=-1, keepdims=True))
    spread = lax.optimization_barrier(jnp.mean((values - centre) ** 2, axis=-1, keepdims=True))
    return (values - centre) * lax.rsqrt(spread + 1e-05)

def project(standardized_activations, weight):
    flat = standardized_activations.reshape(HOMOLOG_CAPACITY * POSITION_TOTAL, EMBED_DIMENSION)
    return jnp.dot(flat, weight, preferred_element_type=jnp.float32).astype(jnp.bfloat16).reshape(HOMOLOG_CAPACITY, POSITION_TOTAL, H, DH)

def column_one(pieces, livef):
    query, key_rows, value_rows = pieces
    scores = jnp.einsum('shd,thd->hst', query.astype(jnp.float32), key_rows.astype(jnp.float32)) / jnp.sqrt(jnp.float32(DH))
    scores = jnp.where(livef[None, None, :] > 0, scores, jnp.float32(-1e+30))
    weights = jax.nn.softmax(scores, axis=-1).astype(jnp.bfloat16)
    result = jnp.einsum('hst,thd->shd', weights.astype(jnp.float32), value_rows.astype(jnp.float32))
    return (result * livef[:, None, None]).astype(jnp.bfloat16)

def reference(embedded_homologs, homolog_tallies, horizontal_probe_matrix, horizontal_lookup_matrix, horizontal_content_matrix, vertical_probe_matrix, vertical_lookup_matrix, vertical_content_matrix):
    count = homolog_tallies[0]
    livef = (jnp.arange(HOMOLOG_CAPACITY, dtype=jnp.int32) < count).astype(jnp.float32)
    standardized_activations = standardize_features(embedded_homologs.astype(jnp.float32)).astype(jnp.bfloat16)
    rq = project(standardized_activations, horizontal_probe_matrix)
    rk = project(standardized_activations, horizontal_lookup_matrix)
    rv = project(standardized_activations, horizontal_content_matrix)
    masked = rq.astype(jnp.float32) * livef[:, None, None, None]
    logits = jnp.einsum('sihd,sjhd->hij', masked, rk.astype(jnp.float32))
    logits = logits / (jnp.sqrt(jnp.float32(DH)) * jnp.sqrt(count.astype(jnp.float32)))
    weights = jax.nn.softmax(logits, axis=-1).astype(jnp.bfloat16)
    horizontal_mixing_result = jnp.einsum('hij,sjhd->sihd', weights.astype(jnp.float32), rv.astype(jnp.float32))
    horizontal_mixing_result = (horizontal_mixing_result * livef[:, None, None, None]).astype(jnp.bfloat16).reshape(HOMOLOG_CAPACITY, POSITION_TOTAL, EMBED_DIMENSION)
    intermediate_activations = embedded_homologs.astype(jnp.float32) + horizontal_mixing_result.astype(jnp.float32)
    normed2 = standardize_features(intermediate_activations).astype(jnp.bfloat16)
    cq = jnp.moveaxis(project(normed2, vertical_probe_matrix), 1, 0)
    ck = jnp.moveaxis(project(normed2, vertical_lookup_matrix), 1, 0)
    cv = jnp.moveaxis(project(normed2, vertical_content_matrix), 1, 0)
    columns = lax.map(lambda pieces: column_one(pieces, livef), (cq, ck, cv))
    column_out = jnp.moveaxis(columns, 0, 1).reshape(HOMOLOG_CAPACITY, POSITION_TOTAL, EMBED_DIMENSION)
    return (horizontal_mixing_result, column_out)
```

```python
import functools
import math

import jax
import jax.numpy as jnp
from jax import lax
from jax.experimental import pallas as pl
from jax.experimental.pallas import tpu as pltpu
from jax.sharding import PartitionSpec as P

H = 12
DH = 64
SEQ = "seq"
LANES = 128
EPS = 1e-05
BF16 = jnp.bfloat16
F32 = jnp.float32
NT = (((1,), (1,)), ((), ()))


def standardize(values):
    centre = jnp.mean(values, axis=-1, keepdims=True)
    shifted = values - centre
    spread = jnp.mean(shifted * shifted, axis=-1, keepdims=True)
    return shifted * lax.rsqrt(spread + EPS)


def half_masks():
    lane = lax.broadcasted_iota(jnp.int32, (1, LANES), 1)
    low = (lane < DH).astype(F32)
    return low.astype(BF16), (1.0 - low).astype(BF16)


def lane_block(value, index):
    return value[:, index * LANES : (index + 1) * LANES]


def logits_kernel(meta, x_ref, wq_ref, wk_ref, normed_ref, logits_ref, total):
    step = pl.program_id(0)
    rows = x_ref.shape[0] // 2
    first, count = meta[0], meta[1]
    normed = standardize(x_ref[...].astype(F32)).astype(BF16)
    normed_ref[...] = normed
    row = lax.broadcasted_iota(jnp.int32, (2 * rows, 1), 0)
    sequence = first + 2 * step + (row >= rows).astype(jnp.int32)
    live = (sequence < count).astype(F32)
    q = (jnp.dot(normed, wq_ref[...], preferred_element_type=F32) * live).astype(BF16)
    k = jnp.dot(normed, wk_ref[...], preferred_element_type=F32).astype(BF16)
    low, high = half_masks()

    @pl.when(step == 0)
    def _():
        total[...] = jnp.zeros_like(total)

    for pair in range(H // 2):
        qp, kp = lane_block(q, pair), lane_block(k, pair)
        both = jnp.concatenate([qp[:rows], qp[rows:]], axis=1)
        even = jnp.concatenate([kp[:rows] * low, kp[rows:] * low], axis=1)
        odd = jnp.concatenate([kp[:rows] * high, kp[rows:] * high], axis=1)
        keys = jnp.concatenate([even, odd], axis=0)
        got = lax.dot_general(both, keys, NT, preferred_element_type=F32)
        at = 2 * pair * rows
        total[at : at + rows, :] += got[:, :rows]
        total[at + rows : at + 2 * rows, :] += got[:, rows:]

    @pl.when(step == pl.num_programs(0) - 1)
    def _():
        logits_ref[...] = total[...].astype(BF16)


def weights_kernel(scale_ref, parts_ref, out_ref):
    logits = parts_ref[0].astype(F32)
    for source in range(1, parts_ref.shape[0]):
        logits += parts_ref[source].astype(F32)
    logits = logits * scale_ref[0]
    top = jnp.max(logits, axis=-1, keepdims=True)
    powers = jnp.exp(logits - top)
    weights = (powers / jnp.sum(powers, axis=-1, keepdims=True)).astype(BF16)
    for target in range(out_ref.shape[0]):
        out_ref[target] = weights


def mix_kernel(meta, w_ref, rv_ref, x_ref, row_ref, *rest):
    sends, held = rest[:-1], rest[-1]
    step = pl.program_id(0)
    rows = x_ref.shape[0] // 2
    first, count = meta[0], meta[1]
    low, high = half_masks()
    mixed = [[], []]
    for pair in range(H // 2):
        at = 2 * pair * rows
        weights = jnp.concatenate([w_ref[at : at + rows, :], w_ref[at + rows : at + 2 * rows, :]], axis=1)
        lanes = slice(pair * LANES, (pair + 1) * LANES)
        values = []
        for s in range(2):
            v = rv_ref[s * rows : (s + 1) * rows, lanes]
            values.append(jnp.concatenate([v * low, v * high], axis=0))
        got = jnp.dot(weights, jnp.concatenate(values, axis=1), preferred_element_type=F32)
        for s in range(2):
            mixed[s].append(lane_block(got, s))
    for s in range(2):
        live = (first + 2 * step + s < count).astype(F32)
        part = slice(s * rows, (s + 1) * rows)
        out = (jnp.concatenate(mixed[s], axis=1) * live).astype(BF16)
        row_ref[part, :] = out
        total = x_ref[part, :].astype(F32) + out.astype(F32)
        held[2 * step + s] = standardize(total)

    @pl.when(step == pl.num_programs(0) - 1)
    def _():
        each = rows // len(sends)
        size = 16
        for k, send in enumerate(sends):
            for block in range(each // size):
                start = k * each + block * size
                turned = jnp.swapaxes(held[:, start : start + size, :], 0, 1)
                flat = turned.reshape(size * held.shape[0], held.shape[2])
                span = size * held.shape[0]
                send[block * span : (block + 1) * span, :] = flat.astype(BF16)


def column_kernel(columns, meta, n_ref, wq_ref, wk_ref, wv_ref, out_ref):
    count = meta[1]
    rows = n_ref.shape[0]
    total = rows // columns
    width = wq_ref.shape[1]
    factor = math.log2(math.e) / math.sqrt(DH)
    n = n_ref[...]
    q = jnp.dot(n, wq_ref[...], preferred_element_type=F32) * factor
    k = jnp.dot(n, wk_ref[...], preferred_element_type=F32)
    v = jnp.dot(n, wv_ref[...], preferred_element_type=F32)
    lane = lax.broadcasted_iota(jnp.int32, (1, LANES), 1)
    low = lane < DH
    first_high = (lane == DH).astype(F32)
    first_low = (lane == 0).astype(F32)
    row = lax.broadcasted_iota(jnp.int32, (total, 1), 0)
    alive = row < count
    bias = jnp.where(alive, 0.0, -1e30).astype(F32)
    live = alive.astype(F32)

    def column(value, c):
        return value.reshape(total // 8, columns, 8, width)[:, c].reshape(total, width)

    results = []
    for c in range(columns):
        qc, kc, vc = column(q, c), column(k, c), column(v, c)
        pieces = []
        for pair in range(width // LANES):
            qp, kp, vp = lane_block(qc, pair), lane_block(kc, pair), lane_block(vc, pair)
            mixes = []
            for even in (True, False):
                if even:
                    qh = jnp.where(low, qp, first_high)
                    kh = jnp.where(low, kp, bias)
                    vh = jnp.where(low, vp, 1.0)
                else:
                    qh = jnp.where(low, first_low, qp)
                    kh = jnp.where(low, bias, kp)
                    vh = jnp.where(low, 1.0, vp)
                scores = lax.dot_general(
                    qh.astype(BF16), kh.astype(BF16), NT, preferred_element_type=F32
                )
                top = jnp.max(scores, axis=-1, keepdims=True)
                powers = jnp.exp2(scores - top).astype(BF16)
                mixes.append(jnp.dot(powers, vh.astype(BF16), preferred_element_type=F32))
            values = jnp.where(low, mixes[0], mixes[1])
            sums = jnp.where(low, mixes[1], mixes[0])
            pieces.append(values * (live / pltpu.roll(sums, DH, 1)))
        results.append(jnp.concatenate(pieces, axis=1))
    if columns > 1:
        stacked = jnp.stack([r.reshape(total // 8, 8, width) for r in results], axis=1)
    else:
        stacked = results[0]
    out_ref[...] = stacked.reshape(rows, width).astype(BF16)


def turn_kernel(recv_ref, out_ref):
    sequences, size = out_ref.shape[0], out_ref.shape[1]
    got = recv_ref[...].astype(F32).reshape(size, sequences, recv_ref.shape[1])
    out_ref[...] = jnp.swapaxes(got, 0, 1).astype(BF16)


def turn_into(recv_ref, kept_ref, out_ref):
    turn_kernel(recv_ref, out_ref)


def row_spec(rows, width):
    return pl.BlockSpec((rows, width), lambda i, *_: (i, 0))


def whole_spec(shape):
    return pl.BlockSpec(shape, lambda i, *_: (0,) * len(shape))


def call(kernel, meta, args, grid, in_specs, out_specs, out_shape, scratch, cost, name):
    return pl.pallas_call(
        kernel,
        grid_spec=pltpu.PrefetchScalarGridSpec(
            num_scalar_prefetch=1,
            grid=grid,
            in_specs=in_specs,
            out_specs=out_specs,
            scratch_shapes=scratch,
        ),
        out_shape=out_shape,
        cost_estimate=cost,
        compiler_params=pltpu.CompilerParams(dimension_semantics=("arbitrary",) * len(grid)),
        name=name,
    )(meta, *args)


CHUNKS = 2


def local(x, tallies, hq, hk, hv, vq, vk, vv):
    sequences, positions, width = x.shape
    groups = lax.axis_size(SEQ)
    tokens = sequences * positions
    count = tallies[0]
    meta = jnp.stack([lax.axis_index(SEQ) * sequences, count]).astype(jnp.int32)
    flat = x.reshape(tokens, width)
    step_rows = 2 * positions
    steps = tokens // step_rows
    share = H * positions // groups

    normed, logits = call(
        logits_kernel,
        meta,
        (flat, hq, hk),
        (steps,),
        [row_spec(step_rows, width), whole_spec((width, width)), whole_spec((width, width))],
        [row_spec(step_rows, width), whole_spec((H * positions, positions))],
        [
            jax.ShapeDtypeStruct((tokens, width), BF16),
            jax.ShapeDtypeStruct((H * positions, positions), BF16),
        ],
        [pltpu.VMEM((H * positions, positions), F32)],
        pl.CostEstimate(flops=4 * tokens * width * width, bytes_accessed=6 << 20, transcendentals=0),
        "row_logits",
    )
    parts = lax.all_to_all(
        logits.reshape(groups, share, positions), SEQ, split_axis=0, concat_axis=0, tiled=True
    )
    rv = jnp.dot(normed, hv, preferred_element_type=F32).astype(BF16)
    scale = (1.0 / (jnp.sqrt(F32(DH)) * jnp.sqrt(count.astype(F32)))).reshape(1)
    copies = pl.pallas_call(
        weights_kernel,
        in_specs=[
            pl.BlockSpec(memory_space=pltpu.SMEM),
            pl.BlockSpec(memory_space=pltpu.VMEM),
        ],
        out_specs=pl.BlockSpec(memory_space=pltpu.VMEM),
        out_shape=jax.ShapeDtypeStruct((groups, share, positions), BF16),
        cost_estimate=pl.CostEstimate(flops=1 << 20, bytes_accessed=1 << 20, transcendentals=0),
        name="row_weights",
    )(scale, parts)
    weights = lax.all_to_all(copies, SEQ, split_axis=0, concat_axis=0, tiled=True)
    weights = weights.reshape(H * positions, positions)

    part_rows = tokens // CHUNKS
    mixed = call(
        mix_kernel,
        meta,
        (weights, rv, flat),
        (steps,),
        [whole_spec((H * positions, positions)), row_spec(step_rows, width), row_spec(step_rows, width)],
        [row_spec(step_rows, width)] + [whole_spec((part_rows, width))] * CHUNKS,
        [jax.ShapeDtypeStruct((tokens, width), BF16)]
        + [jax.ShapeDtypeStruct((part_rows, width), BF16)] * CHUNKS,
        [pltpu.VMEM((sequences, positions, width), F32)],
        pl.CostEstimate(flops=4 * tokens * width * positions, bytes_accessed=8 << 20, transcendentals=0),
        "row_mix",
    )
    row_out, sends = mixed[0], mixed[1:]

    columns = positions // groups // CHUNKS
    lanes = 2 * LANES
    each = positions // CHUNKS
    returned = []
    arrived = [
        lax.all_to_all(
            s.reshape(groups, part_rows // groups, width), SEQ, split_axis=0, concat_axis=0, tiled=True
        )
        for s in sends
    ]
    for got in arrived:
        out = call(
            functools.partial(column_kernel, columns),
            meta,
            (got.reshape(part_rows, width), vq, vk, vv),
            (width // lanes,),
            [whole_spec((part_rows, width))]
            + [pl.BlockSpec((width, lanes), lambda i, *_: (0, i))] * 3,
            pl.BlockSpec((part_rows, lanes), lambda i, *_: (0, i)),
            jax.ShapeDtypeStruct((part_rows, width), BF16),
            [],
            pl.CostEstimate(
                flops=6 * part_rows * width * width, bytes_accessed=6 << 20, transcendentals=0
            ),
            "columns",
        )
        returned.append(
            lax.all_to_all(
                out.reshape(groups, part_rows // groups, width),
                SEQ,
                split_axis=0,
                concat_axis=0,
                tiled=True,
            )
        )
    result = None
    block = 16
    count_blocks = each // block
    for k, got in enumerate(returned):
        args = [got.reshape(part_rows, width)]
        in_specs = [pl.BlockSpec((block * sequences, width), lambda i: (i, 0))]
        if k > 0:
            args.append(result)
            in_specs.append(pl.BlockSpec(memory_space=pl.ANY))
        result = pl.pallas_call(
            turn_kernel if k == 0 else turn_into,
            grid=(count_blocks,),
            in_specs=in_specs,
            out_specs=pl.BlockSpec(
                (sequences, block, width), lambda i, k=k: (0, k * count_blocks + i, 0)
            ),
            out_shape=jax.ShapeDtypeStruct((sequences, positions, width), BF16),
            input_output_aliases={} if k == 0 else {1: 0},
            cost_estimate=pl.CostEstimate(flops=0, bytes_accessed=3 << 20, transcendentals=0),
            name="turn_back",
        )(*args)
    return row_out.reshape(sequences, positions, width), result


def solution(mesh):
    whole = P(("aln", "seq"), None, None)
    in_specs = (whole, P("aln"), P(), P(), P(), P(), P(), P())
    return jax.shard_map(
        local, mesh=mesh, in_specs=in_specs, out_specs=(whole, whole), check_vma=False
    )
```

```python
import functools
import math

import jax
import jax.numpy as jnp
from jax import lax
from jax.experimental import pallas as pl
from jax.experimental.pallas import tpu as pltpu
from jax.sharding import PartitionSpec as P

H = 12
DH = 64
SEQ = "seq"
LANES = 128
EPS = 1e-05
BF16 = jnp.bfloat16
F32 = jnp.float32
NT = (((1,), (1,)), ((), ()))


def standardize(values):
    centre = jnp.mean(values, axis=-1, keepdims=True)
    shifted = values - centre
    spread = jnp.mean(shifted * shifted, axis=-1, keepdims=True)
    return shifted * lax.rsqrt(spread + EPS)


def half_masks():
    lane = lax.broadcasted_iota(jnp.int32, (1, LANES), 1)
    low = (lane < DH).astype(F32)
    return low.astype(BF16), (1.0 - low).astype(BF16)


def lane_block(value, index):
    return value[:, index * LANES : (index + 1) * LANES]


def logits_kernel(tally, x_ref, wq_ref, wk_ref, wv_ref, rv_ref, logits_ref, total):
    step = pl.program_id(0)
    rows = x_ref.shape[0] // 2
    first, count = lax.axis_index(SEQ) * (2 * pl.num_programs(0)), tally[0]

    @pl.when((step == 0) & (lax.rem(lax.axis_index("aln"), 2) == 1))
    def _():
        pl.delay(STAGGER)

    normed = standardize(x_ref[...].astype(F32)).astype(BF16)
    row = lax.broadcasted_iota(jnp.int32, (2 * rows, 1), 0)
    sequence = first + 2 * step + (row >= rows).astype(jnp.int32)
    live = (sequence < count).astype(F32)
    q = (jnp.dot(normed, wq_ref[...], preferred_element_type=F32) * live).astype(BF16)
    k = jnp.dot(normed, wk_ref[...], preferred_element_type=F32).astype(BF16)
    rv_ref[...] = jnp.dot(normed, wv_ref[...], preferred_element_type=F32).astype(BF16)
    low, high = half_masks()

    @pl.when(step == 0)
    def _():
        total[...] = jnp.zeros_like(total)

    for pair in range(H // 2):
        qp, kp = lane_block(q, pair), lane_block(k, pair)
        both = jnp.concatenate([qp[:rows], qp[rows:]], axis=1)
        even = jnp.concatenate([kp[:rows] * low, kp[rows:] * low], axis=1)
        odd = jnp.concatenate([kp[:rows] * high, kp[rows:] * high], axis=1)
        keys = jnp.concatenate([even, odd], axis=0)
        got = lax.dot_general(both, keys, NT, preferred_element_type=F32)
        at = 2 * pair * rows
        total[at : at + rows, :] += got[:, :rows]
        total[at + rows : at + 2 * rows, :] += got[:, rows:]

    @pl.when(step == pl.num_programs(0) - 1)
    def _():
        logits_ref[...] = total[...].astype(BF16)


def weights_kernel(tally, parts_ref, out_ref):
    logits = parts_ref[0].astype(F32)
    for source in range(1, parts_ref.shape[0]):
        logits += parts_ref[source].astype(F32)
    count = jnp.full((1, 1), tally[0], jnp.int32).astype(F32)
    logits = logits / (jnp.sqrt(F32(DH)) * jnp.sqrt(count))
    top = jnp.max(logits, axis=-1, keepdims=True)
    powers = jnp.exp(logits - top)
    weights = (powers / jnp.sum(powers, axis=-1, keepdims=True)).astype(BF16)
    for target in range(out_ref.shape[0]):
        out_ref[target] = weights


def mix_kernel(tally, w_ref, rv_ref, x_ref, row_ref, *rest):
    sends, held = rest[:-1], rest[-1]
    step = pl.program_id(0)
    rows = x_ref.shape[0] // 2
    first, count = lax.axis_index(SEQ) * held.shape[0], tally[0]
    low, high = half_masks()
    mixed = [[], []]
    for pair in range(H // 2):
        at = 2 * pair * rows
        weights = jnp.concatenate([w_ref[at : at + rows, :], w_ref[at + rows : at + 2 * rows, :]], axis=1)
        lanes = slice(pair * LANES, (pair + 1) * LANES)
        values = []
        for s in range(2):
            v = rv_ref[s * rows : (s + 1) * rows, lanes]
            values.append(jnp.concatenate([v * low, v * high], axis=0))
        got = jnp.dot(weights, jnp.concatenate(values, axis=1), preferred_element_type=F32)
        for s in range(2):
            mixed[s].append(lane_block(got, s))
    for s in range(2):
        live = (first + 2 * step + s < count).astype(F32)
        part = slice(s * rows, (s + 1) * rows)
        out = (jnp.concatenate(mixed[s], axis=1) * live).astype(BF16)
        row_ref[part, :] = out
        total = x_ref[part, :].astype(F32) + out.astype(F32)
        held[2 * step + s] = standardize(total)

    @pl.when(step == pl.num_programs(0) - 1)
    def _():
        each = rows // len(sends)
        size = 16
        for k, send in enumerate(sends):
            for block in range(each // size):
                start = k * each + block * size
                turned = jnp.swapaxes(held[:, start : start + size, :], 0, 1)
                flat = turned.reshape(size * held.shape[0], held.shape[2])
                span = size * held.shape[0]
                send[block * span : (block + 1) * span, :] = flat.astype(BF16)


def column_kernel(columns, tally, n_ref, wq_ref, wk_ref, wv_ref, out_ref):
    count = tally[0]
    rows = n_ref.shape[0]
    total = rows // columns
    width = wq_ref.shape[1]
    factor = math.log2(math.e) / math.sqrt(DH)
    n = n_ref[...]
    q = jnp.dot(n, wq_ref[...], preferred_element_type=F32) * factor
    k = jnp.dot(n, wk_ref[...], preferred_element_type=F32)
    v = jnp.dot(n, wv_ref[...], preferred_element_type=F32)
    lane = lax.broadcasted_iota(jnp.int32, (1, LANES), 1)
    low = lane < DH
    first_high = (lane == DH).astype(F32)
    first_low = (lane == 0).astype(F32)
    row = lax.broadcasted_iota(jnp.int32, (total, 1), 0)
    alive = row < count
    bias = jnp.where(alive, 0.0, -1e30).astype(F32)
    live = alive.astype(F32)

    def column(value, c):
        return value.reshape(total // 8, columns, 8, width)[:, c].reshape(total, width)

    results = []
    for c in range(columns):
        qc, kc, vc = column(q, c), column(k, c), column(v, c)
        pieces = []
        for pair in range(width // LANES):
            qp, kp, vp = lane_block(qc, pair), lane_block(kc, pair), lane_block(vc, pair)
            mixes = []
            for even in (True, False):
                if even:
                    qh = jnp.where(low, qp, first_high)
                    kh = jnp.where(low, kp, bias)
                    vh = jnp.where(low, vp, 1.0)
                else:
                    qh = jnp.where(low, first_low, qp)
                    kh = jnp.where(low, bias, kp)
                    vh = jnp.where(low, 1.0, vp)
                scores = lax.dot_general(
                    qh.astype(BF16), kh.astype(BF16), NT, preferred_element_type=F32
                )
                top = jnp.max(scores, axis=-1, keepdims=True)
                powers = jnp.exp2(scores - top).astype(BF16)
                mixes.append(jnp.dot(powers, vh.astype(BF16), preferred_element_type=F32))
            values = jnp.where(low, mixes[0], mixes[1])
            sums = jnp.where(low, mixes[1], mixes[0])
            pieces.append(values * (live / pltpu.roll(sums, DH, 1)))
        results.append(jnp.concatenate(pieces, axis=1))
    if columns > 1:
        stacked = jnp.stack([r.reshape(total // 8, 8, width) for r in results], axis=1)
    else:
        stacked = results[0]
    out_ref[...] = stacked.reshape(rows, width).astype(BF16)


def row_spec(rows, width):
    return pl.BlockSpec((rows, width), lambda i, *_: (i, 0))


def whole_spec(shape):
    return pl.BlockSpec(shape, lambda i, *_: (0,) * len(shape))


def call(kernel, meta, args, grid, in_specs, out_specs, out_shape, scratch, cost, name, vmem):
    return pl.pallas_call(
        kernel,
        grid_spec=pltpu.PrefetchScalarGridSpec(
            num_scalar_prefetch=1,
            grid=grid,
            in_specs=in_specs,
            out_specs=out_specs,
            scratch_shapes=scratch,
        ),
        out_shape=out_shape,
        cost_estimate=cost,
        compiler_params=pltpu.CompilerParams(
            dimension_semantics=("arbitrary",) * len(grid), vmem_limit_bytes=vmem << 20
        ),
        name=name,
    )(meta, *args)


STAGGER = 22000


def exchange(value):
    return lax.all_to_all(value, SEQ, split_axis=0, concat_axis=0, tiled=True)


def in_hbm(*arrays):
    return tuple(pltpu.with_memory_space_constraint(a, pltpu.HBM) for a in arrays)


def local(x, tallies, hq, hk, hv, vq, vk, vv):
    sequences, positions, width = x.shape
    groups = lax.axis_size(SEQ)
    tokens = sequences * positions
    flat = x.reshape(tokens, width)
    step_rows = 2 * positions
    steps = tokens // step_rows
    share = H * positions // groups

    rv, logits = call(
        logits_kernel,
        tallies,
        in_hbm(flat, hq, hk, hv),
        (steps,),
        [row_spec(step_rows, width)] + [whole_spec((width, width))] * 3,
        [row_spec(step_rows, width), whole_spec((H * positions, positions))],
        [
            jax.ShapeDtypeStruct((tokens, width), BF16),
            jax.ShapeDtypeStruct((H * positions, positions), BF16),
        ],
        [pltpu.VMEM((H * positions, positions), F32)],
        pl.CostEstimate(flops=6 * tokens * width * width, bytes_accessed=6 << 20, transcendentals=0),
        "row_logits",
        24,
    )
    parts = exchange(logits.reshape(groups, share, positions))
    copies = pl.pallas_call(
        weights_kernel,
        in_specs=[
            pl.BlockSpec(memory_space=pltpu.SMEM),
            pl.BlockSpec(memory_space=pltpu.VMEM),
        ],
        out_specs=pl.BlockSpec(memory_space=pltpu.VMEM),
        out_shape=jax.ShapeDtypeStruct((groups, share, positions), BF16),
        cost_estimate=pl.CostEstimate(flops=1 << 20, bytes_accessed=1 << 20, transcendentals=0),
        compiler_params=pltpu.CompilerParams(vmem_limit_bytes=8 << 20),
        name="row_weights",
    )(tallies, parts)
    weights = exchange(copies).reshape(H * positions, positions)
    rv, flat = in_hbm(rv, flat)
    row_out, send = call(
        mix_kernel,
        tallies,
        (weights, rv, flat),
        (steps,),
        [whole_spec((H * positions, positions)), row_spec(step_rows, width), row_spec(step_rows, width)],
        [row_spec(step_rows, width), whole_spec((tokens, width))],
        [jax.ShapeDtypeStruct((tokens, width), BF16)] * 2,
        [pltpu.VMEM((sequences, positions, width), F32)],
        pl.CostEstimate(flops=4 * tokens * width * positions, bytes_accessed=8 << 20, transcendentals=0),
        "row_mix",
        24,
    )
    columns = positions // groups
    lanes = 2 * LANES
    got = exchange(send.reshape(groups, tokens // groups, width)).reshape(tokens, width)
    out = call(
        functools.partial(column_kernel, columns),
        tallies,
        (got, vq, vk, vv),
        (width // lanes,),
        [whole_spec((tokens, width))] + [pl.BlockSpec((width, lanes), lambda i, *_: (0, i))] * 3,
        pl.BlockSpec((tokens, lanes), lambda i, *_: (0, i)),
        jax.ShapeDtypeStruct((tokens, width), BF16),
        [],
        pl.CostEstimate(flops=6 * tokens * width * width, bytes_accessed=6 << 20, transcendentals=0),
        "columns",
        40,
    )
    back = exchange(out.reshape(groups, tokens // groups, width))
    result = jnp.swapaxes(back.reshape(positions, sequences, width), 0, 1)
    return row_out.reshape(sequences, positions, width), result


def solution(mesh):
    whole = P(("aln", "seq"), None, None)
    in_specs = (whole, P("aln"), P(), P(), P(), P(), P(), P())
    return jax.shard_map(
        local, mesh=mesh, in_specs=in_specs, out_specs=(whole, whole), check_vma=False
    )
```

```python
import math

import jax
import jax.numpy as jnp
from jax import lax
from jax.experimental import pallas as pl
from jax.experimental.pallas import tpu as pltpu
from jax.sharding import PartitionSpec as P

H = 12
DH = 64
SEQ = "seq"
LANES = 128
EPS = 1e-05
BF16 = jnp.bfloat16
F32 = jnp.float32
NT = (((1,), (1,)), ((), ()))


def standardize(values):
    centre = jnp.mean(values, axis=-1, keepdims=True)
    shifted = values - centre
    spread = jnp.mean(shifted * shifted, axis=-1, keepdims=True)
    return shifted * lax.rsqrt(spread + EPS)


def half_masks():
    lane = lax.broadcasted_iota(jnp.int32, (1, LANES), 1)
    low = (lane < DH).astype(F32)
    return low.astype(BF16), (1.0 - low).astype(BF16)


def lane_block(value, index):
    return value[:, index * LANES : (index + 1) * LANES]


def fetch(refs, sems):
    copies = [pltpu.make_async_copy(src, dst, sems.at[i]) for i, (src, dst) in enumerate(refs)]
    for copy in copies:
        copy.start()
    return copies


def logits_kernel(
    tally, x_hbm, wq_hbm, wk_hbm, wv_hbm, rv_ref, logits_ref, x_ref, wq_ref, wk_ref, wv_ref, n_ref, q_ref, k_ref, sems
):
    @pl.when(lax.rem(lax.axis_index("aln"), 2) == 1)
    def _():
        pl.delay(STAGGER)

    copies = fetch(
        ((x_hbm, x_ref), (wq_hbm, wq_ref), (wk_hbm, wk_ref), (wv_hbm, wv_ref)), sems
    )
    tokens = x_ref.shape[0]
    positions = logits_ref.shape[1]
    sequences = tokens // positions
    first, count = lax.axis_index(SEQ) * sequences, tally[0]
    copies[0].wait()
    for s in range(sequences):
        part = slice(s * positions, (s + 1) * positions)
        n_ref[part, :] = standardize(x_ref[part, :].astype(F32)).astype(BF16)
    size = 2 * positions
    copies[1].wait()
    for start in range(0, tokens, size):
        part = slice(start, start + size)
        q = jnp.dot(n_ref[part, :], wq_ref[...], preferred_element_type=F32)
        for s in range(2):
            at = start + s * positions
            live = (first + at // positions < count).astype(F32)
            q_ref[at : at + positions, :] = (q[s * positions : (s + 1) * positions] * live).astype(BF16)
    copies[2].wait()
    for start in range(0, tokens, size):
        part = slice(start, start + size)
        k_ref[part, :] = jnp.dot(n_ref[part, :], wk_ref[...], preferred_element_type=F32).astype(BF16)
    copies[3].wait()
    for start in range(0, tokens, size):
        part = slice(start, start + size)
        rv_ref[part, :] = jnp.dot(n_ref[part, :], wv_ref[...], preferred_element_type=F32).astype(BF16)
    low, high = half_masks()
    for pair in range(H // 2):
        lanes = slice(pair * LANES, (pair + 1) * LANES)
        got = None
        for s in range(0, sequences, 2):
            rows = [slice((s + e) * positions, (s + e + 1) * positions) for e in range(2)]
            queries = jnp.concatenate([q_ref[r, lanes] for r in rows], axis=1)
            keys = [k_ref[r, lanes] for r in rows]
            even = jnp.concatenate([k * low for k in keys], axis=1)
            odd = jnp.concatenate([k * high for k in keys], axis=1)
            term = lax.dot_general(
                queries, jnp.concatenate([even, odd], axis=0), NT, preferred_element_type=F32
            )
            got = term if got is None else got + term
        at = 2 * pair * positions
        logits_ref[at : at + positions, :] = got[:, :positions].astype(BF16)
        logits_ref[at + positions : at + 2 * positions, :] = got[:, positions:].astype(BF16)


def weights_kernel(tally, parts_ref, out_ref):
    logits = parts_ref[0].astype(F32)
    for source in range(1, parts_ref.shape[0]):
        logits += parts_ref[source].astype(F32)
    count = jnp.full((1, 1), tally[0], jnp.int32).astype(F32)
    logits = logits / (jnp.sqrt(F32(DH)) * jnp.sqrt(count))
    top = jnp.max(logits, axis=-1, keepdims=True)
    powers = jnp.exp(logits - top)
    weights = (powers / jnp.sum(powers, axis=-1, keepdims=True)).astype(BF16)
    for target in range(out_ref.shape[0]):
        out_ref[target] = weights


def mix_kernel(tally, w_ref, rv_ref, x_ref, row_ref, send_ref, held):
    sequences, positions, width = held.shape
    first, count = lax.axis_index(SEQ) * sequences, tally[0]
    low, high = half_masks()
    for start in range(0, sequences, 2):
        mixed = [[], []]
        for pair in range(H // 2):
            at = 2 * pair * positions
            weights = jnp.concatenate(
                [w_ref[at : at + positions, :], w_ref[at + positions : at + 2 * positions, :]], axis=1
            )
            lanes = slice(pair * LANES, (pair + 1) * LANES)
            values = []
            for s in range(2):
                v = rv_ref[(start + s) * positions : (start + s + 1) * positions, lanes]
                values.append(jnp.concatenate([v * low, v * high], axis=0))
            got = jnp.dot(weights, jnp.concatenate(values, axis=1), preferred_element_type=F32)
            for s in range(2):
                mixed[s].append(lane_block(got, s))
        for s in range(2):
            live = (first + start + s < count).astype(F32)
            part = slice((start + s) * positions, (start + s + 1) * positions)
            out = (jnp.concatenate(mixed[s], axis=1) * live).astype(BF16)
            row_ref[part, :] = out
            held[start + s] = standardize(x_ref[part, :].astype(F32) + out.astype(F32))
    size = 16
    span = size * sequences
    for block in range(positions // size):
        turned = jnp.swapaxes(held[:, block * size : (block + 1) * size, :], 0, 1)
        send_ref[block * span : (block + 1) * span, :] = turned.reshape(span, width).astype(BF16)


def column_kernel(tally, n_ref, wq_ref, wk_ref, wv_ref, out_ref, q_ref, k_ref, v_ref):
    rows, width = n_ref.shape
    sets, columns, total, lanes = q_ref.shape
    factor = math.log2(math.e) / math.sqrt(DH)
    low, high = half_masks()
    lane = lax.broadcasted_iota(jnp.int32, (1, LANES), 1)
    is_low = lane < DH
    one_high = (lane == DH).astype(F32).astype(BF16)
    one_low = (lane == 0).astype(F32).astype(BF16)
    alive = lax.broadcasted_iota(jnp.int32, (total, 1), 0) < tally[0]
    bias = jnp.where(alive, 0.0, -1e30).astype(F32)
    bias_high = jnp.where(is_low, 0.0, bias).astype(BF16)
    bias_low = jnp.where(is_low, bias, 0.0).astype(BF16)
    live = alive.astype(F32)
    size = 256
    each = size // (8 * columns)

    def project(part, start, source, target, scale):
        got = jnp.dot(
            n_ref[start : start + size, :],
            source[:, part * lanes : (part + 1) * lanes],
            preferred_element_type=F32,
        )
        if scale is not None:
            got = got * scale
        got = got.reshape(each, columns, 8, lanes)
        at = start // columns
        for c in range(columns):
            target[part, c, at : at + each * 8, :] = got[:, c].reshape(each * 8, lanes).astype(BF16)

    def mix(q, k, v):
        scores = lax.dot_general(q, k, NT, preferred_element_type=F32)
        powers = jnp.exp2(scores - jnp.max(scores, axis=-1, keepdims=True)).astype(BF16)
        return jnp.dot(powers, v, preferred_element_type=F32)

    def attend(part, first, pair):
        outs = []
        span = slice(pair * LANES, (pair + 1) * LANES)
        for c in (first, first + 1):
            q, k, v = q_ref[part, c, :, span], k_ref[part, c, :, span], v_ref[part, c, :, span]
            even = mix(q * low + one_high, k * low + bias_high, v * low + high)
            odd = mix(q * high + one_low, k * high + bias_low, v * high + low)
            values = jnp.where(is_low, even, odd)
            sums = jnp.where(is_low, odd, even)
            outs.append((values * (live / pltpu.roll(sums, DH, 1))).reshape(total // 8, 8, LANES))
        at = part * lanes + pair * LANES
        both = jnp.stack(outs, axis=1).reshape(total // 8, 16, LANES)
        out_ref[:, first // 2, :, at : at + LANES] = both.astype(BF16)

    for part in range(sets):
        for start in range(0, rows, size):
            project(part, start, wq_ref, q_ref, factor)
            project(part, start, wk_ref, k_ref, None)
            project(part, start, wv_ref, v_ref, None)
        for first in range(0, columns, 2):
            for pair in range(lanes // LANES):
                attend(part, first, pair)


def call(kernel, tally, args, spaces, shapes, scratch, flops, name):
    specs = [pl.BlockSpec(memory_space=pltpu.SMEM)]
    return pl.pallas_call(
        kernel,
        in_specs=specs + [pl.BlockSpec(memory_space=s) for s in spaces],
        out_specs=[pl.BlockSpec(memory_space=pltpu.VMEM)] * len(shapes),
        out_shape=[jax.ShapeDtypeStruct(s, BF16) for s in shapes],
        scratch_shapes=scratch,
        cost_estimate=pl.CostEstimate(flops=flops, bytes_accessed=6 << 20, transcendentals=0),
        compiler_params=pltpu.CompilerParams(vmem_limit_bytes=24 << 20),
        name=name,
    )(tally, *args)


STAGGER = 20000


def exchange(value):
    return lax.all_to_all(value, SEQ, split_axis=0, concat_axis=0, tiled=True)


def local(x, tallies, hq, hk, hv, vq, vk, vv):
    sequences, positions, width = x.shape
    groups = lax.axis_size(SEQ)
    tokens = sequences * positions
    flat = x.reshape(tokens, width)
    share = H * positions // groups
    square = pltpu.VMEM((width, width), BF16)
    block = pltpu.VMEM((tokens, width), BF16)

    rv, logits = call(
        logits_kernel,
        tallies,
        tuple(pltpu.with_memory_space_constraint(a, pltpu.HBM) for a in (flat, hq, hk, hv)),
        [pltpu.HBM] * 4,
        [(tokens, width), (H * positions, positions)],
        [block, square, square, square, block, block, block, pltpu.SemaphoreType.DMA((4,))],
        6 * tokens * width * width,
        "row_logits",
    )
    parts = exchange(logits.reshape(groups, share, positions))
    (copies,) = call(
        weights_kernel,
        tallies,
        (parts,),
        [pltpu.VMEM],
        [(groups, share, positions)],
        [],
        1 << 20,
        "row_weights",
    )
    weights = exchange(copies).reshape(H * positions, positions)
    row_out, send = call(
        mix_kernel,
        tallies,
        (weights, rv, flat),
        [pltpu.VMEM] * 3,
        [(tokens, width)] * 2,
        [pltpu.VMEM((sequences, positions, width), F32)],
        4 * tokens * width * positions,
        "row_mix",
    )
    columns = positions // groups
    lanes = 2 * LANES
    got = exchange(send.reshape(groups, tokens // groups, width)).reshape(tokens, width)
    (out,) = call(
        column_kernel,
        tallies,
        (got, vq, vk, vv),
        [pltpu.VMEM] * 4,
        [(groups, columns // 2, 16, width)],
        [pltpu.VMEM((width // lanes, columns, tokens // columns, lanes), BF16)] * 3,
        6 * tokens * width * width,
        "columns",
    )
    back = exchange(out.reshape(groups, tokens // groups, width))
    result = jnp.swapaxes(back.reshape(positions, sequences, width), 0, 1)
    return row_out.reshape(sequences, positions, width), result


def solution(mesh):
    whole = P(("aln", "seq"), None, None)
    in_specs = (whole, P("aln"), P(), P(), P(), P(), P(), P())
    return jax.shard_map(
        local, mesh=mesh, in_specs=in_specs, out_specs=(whole, whole), check_vma=False
    )
```

```python
import math

import jax
import jax.numpy as jnp
from jax import lax
from jax.experimental import pallas as pl
from jax.experimental.pallas import tpu as pltpu
from jax.sharding import PartitionSpec as P

H = 12
DH = 64
SEQ = "seq"
LANES = 128
EPS = 1e-05
BF16 = jnp.bfloat16
F32 = jnp.float32
NT = (((1,), (1,)), ((), ()))


def standardize(values):
    centre = jnp.mean(values, axis=-1, keepdims=True)
    shifted = values - centre
    spread = jnp.mean(shifted * shifted, axis=-1, keepdims=True)
    return shifted * lax.rsqrt(spread + EPS)


def half_masks():
    lane = lax.broadcasted_iota(jnp.int32, (1, LANES), 1)
    low = (lane < DH).astype(F32)
    return low.astype(BF16), (1.0 - low).astype(BF16)


def lane_block(value, index):
    return value[:, index * LANES : (index + 1) * LANES]


def hold_second_core(duration):
    @pl.when(lax.rem(lax.axis_index("aln"), 2) == 1)
    def _():
        pl.delay(duration)


def fetch(refs, sems):
    copies = [pltpu.make_async_copy(src, dst, sems.at[i]) for i, (src, dst) in enumerate(refs)]
    for copy in copies:
        copy.start()
    return copies


def logits_kernel(
    tally, x_hbm, wq_hbm, wk_hbm, wv_hbm, rv_ref, logits_ref, x_ref, wq_ref, wk_ref, wv_ref, n_ref, q_ref, k_ref, sems
):
    hold_second_core(FIRST_STAGGER)
    copies = fetch(
        ((x_hbm, x_ref), (wq_hbm, wq_ref), (wk_hbm, wk_ref), (wv_hbm, wv_ref)), sems
    )
    tokens = x_ref.shape[0]
    positions = logits_ref.shape[1]
    sequences = tokens // positions
    first, count = lax.axis_index(SEQ) * sequences, tally[0]
    copies[0].wait()
    for s in range(sequences):
        part = slice(s * positions, (s + 1) * positions)
        n_ref[part, :] = standardize(x_ref[part, :].astype(F32)).astype(BF16)
    size = 2 * positions
    copies[1].wait()
    for start in range(0, tokens, size):
        part = slice(start, start + size)
        q = jnp.dot(n_ref[part, :], wq_ref[...], preferred_element_type=F32)
        for s in range(2):
            at = start + s * positions
            live = (first + at // positions < count).astype(F32)
            q_ref[at : at + positions, :] = (q[s * positions : (s + 1) * positions] * live).astype(BF16)
    copies[2].wait()
    for start in range(0, tokens, size):
        part = slice(start, start + size)
        k_ref[part, :] = jnp.dot(n_ref[part, :], wk_ref[...], preferred_element_type=F32).astype(BF16)
    copies[3].wait()
    for start in range(0, tokens, size):
        part = slice(start, start + size)
        rv_ref[part, :] = jnp.dot(n_ref[part, :], wv_ref[...], preferred_element_type=F32).astype(BF16)
    low, high = half_masks()
    for pair in range(H // 2):
        lanes = slice(pair * LANES, (pair + 1) * LANES)
        got = None
        for s in range(0, sequences, 2):
            rows = [slice((s + e) * positions, (s + e + 1) * positions) for e in range(2)]
            queries = jnp.concatenate([q_ref[r, lanes] for r in rows], axis=1)
            keys = [k_ref[r, lanes] for r in rows]
            even = jnp.concatenate([k * low for k in keys], axis=1)
            odd = jnp.concatenate([k * high for k in keys], axis=1)
            term = lax.dot_general(
                queries, jnp.concatenate([even, odd], axis=0), NT, preferred_element_type=F32
            )
            got = term if got is None else got + term
        at = 2 * pair * positions
        logits_ref[at : at + positions, :] = got[:, :positions].astype(BF16)
        logits_ref[at + positions : at + 2 * positions, :] = got[:, positions:].astype(BF16)


def weights_kernel(tally, parts_ref, out_ref):
    logits = parts_ref[0].astype(F32)
    for source in range(1, parts_ref.shape[0]):
        logits += parts_ref[source].astype(F32)
    count = jnp.full((1, 1), tally[0], jnp.int32).astype(F32)
    logits = logits / (jnp.sqrt(F32(DH)) * jnp.sqrt(count))
    top = jnp.max(logits, axis=-1, keepdims=True)
    powers = jnp.exp(logits - top)
    weights = (powers / jnp.sum(powers, axis=-1, keepdims=True)).astype(BF16)
    for target in range(out_ref.shape[0]):
        out_ref[target] = weights


def mix_kernel(tally, w_ref, rv_ref, x_ref, row_ref, send_ref, held):
    hold_second_core(SECOND_STAGGER)
    sequences, positions, width = held.shape
    first, count = lax.axis_index(SEQ) * sequences, tally[0]
    low, high = half_masks()
    for start in range(0, sequences, 2):
        mixed = [[], []]
        for pair in range(H // 2):
            at = 2 * pair * positions
            weights = jnp.concatenate(
                [w_ref[at : at + positions, :], w_ref[at + positions : at + 2 * positions, :]], axis=1
            )
            lanes = slice(pair * LANES, (pair + 1) * LANES)
            values = []
            for s in range(2):
                v = rv_ref[(start + s) * positions : (start + s + 1) * positions, lanes]
                values.append(jnp.concatenate([v * low, v * high], axis=0))
            got = jnp.dot(weights, jnp.concatenate(values, axis=1), preferred_element_type=F32)
            for s in range(2):
                mixed[s].append(lane_block(got, s))
        for s in range(2):
            live = (first + start + s < count).astype(F32)
            part = slice((start + s) * positions, (start + s + 1) * positions)
            out = (jnp.concatenate(mixed[s], axis=1) * live).astype(BF16)
            row_ref[part, :] = out
            held[start + s] = standardize(x_ref[part, :].astype(F32) + out.astype(F32))
    size = 16
    span = size * sequences
    for block in range(positions // size):
        turned = jnp.swapaxes(held[:, block * size : (block + 1) * size, :], 0, 1)
        send_ref[block * span : (block + 1) * span, :] = turned.reshape(span, width).astype(BF16)


def column_kernel(tally, n_ref, wq_ref, wk_ref, wv_ref, out_ref, q_ref, k_ref, v_ref):
    rows, width = n_ref.shape
    sets, columns, total, lanes = q_ref.shape
    factor = math.log2(math.e) / math.sqrt(DH)
    low, high = half_masks()
    lane = lax.broadcasted_iota(jnp.int32, (1, LANES), 1)
    is_low = lane < DH
    one_high = (lane == DH).astype(F32).astype(BF16)
    one_low = (lane == 0).astype(F32).astype(BF16)
    alive = lax.broadcasted_iota(jnp.int32, (total, 1), 0) < tally[0]
    bias = jnp.where(alive, 0.0, -1e30).astype(F32)
    bias_high = jnp.where(is_low, 0.0, bias).astype(BF16)
    bias_low = jnp.where(is_low, bias, 0.0).astype(BF16)
    live = alive.astype(F32)
    size = 256
    each = size // (8 * columns)

    def project(part, start, source, target, scale):
        got = jnp.dot(
            n_ref[start : start + size, :],
            source[:, part * lanes : (part + 1) * lanes],
            preferred_element_type=F32,
        )
        if scale is not None:
            got = got * scale
        got = got.reshape(each, columns, 8, lanes)
        at = start // columns
        for c in range(columns):
            target[part, c, at : at + each * 8, :] = got[:, c].reshape(each * 8, lanes).astype(BF16)

    def mix(q, k, v):
        scores = lax.dot_general(q, k, NT, preferred_element_type=F32)
        powers = jnp.exp2(scores - jnp.max(scores, axis=-1, keepdims=True)).astype(BF16)
        return jnp.dot(powers, v, preferred_element_type=F32)

    def attend(part, first, pair):
        outs = []
        span = slice(pair * LANES, (pair + 1) * LANES)
        for c in (first, first + 1):
            q, k, v = q_ref[part, c, :, span], k_ref[part, c, :, span], v_ref[part, c, :, span]
            even = mix(q * low + one_high, k * low + bias_high, v * low + high)
            odd = mix(q * high + one_low, k * high + bias_low, v * high + low)
            values = jnp.where(is_low, even, odd)
            sums = jnp.where(is_low, odd, even)
            outs.append((values * (live / pltpu.roll(sums, DH, 1))).reshape(total // 8, 8, LANES))
        at = part * lanes + pair * LANES
        both = jnp.stack(outs, axis=1).reshape(total // 8, 16, LANES)
        out_ref[:, first // 2, :, at : at + LANES] = both.astype(BF16)

    for part in range(sets):
        for start in range(0, rows, size):
            project(part, start, wq_ref, q_ref, factor)
            project(part, start, wk_ref, k_ref, None)
            project(part, start, wv_ref, v_ref, None)
        for first in range(0, columns, 2):
            for pair in range(lanes // LANES):
                attend(part, first, pair)


def call(kernel, tally, args, spaces, shapes, scratch, flops, name):
    specs = [pl.BlockSpec(memory_space=pltpu.SMEM)]
    return pl.pallas_call(
        kernel,
        in_specs=specs + [pl.BlockSpec(memory_space=s) for s in spaces],
        out_specs=[pl.BlockSpec(memory_space=pltpu.VMEM)] * len(shapes),
        out_shape=[jax.ShapeDtypeStruct(s, BF16) for s in shapes],
        scratch_shapes=scratch,
        cost_estimate=pl.CostEstimate(flops=flops, bytes_accessed=6 << 20, transcendentals=0),
        compiler_params=pltpu.CompilerParams(vmem_limit_bytes=24 << 20),
        name=name,
    )(tally, *args)


FIRST_STAGGER = 10500
SECOND_STAGGER = 11500


def exchange(value):
    return lax.all_to_all(value, SEQ, split_axis=0, concat_axis=0, tiled=True)


def local(x, tallies, hq, hk, hv, vq, vk, vv):
    sequences, positions, width = x.shape
    groups = lax.axis_size(SEQ)
    tokens = sequences * positions
    flat = x.reshape(tokens, width)
    share = H * positions // groups
    square = pltpu.VMEM((width, width), BF16)
    block = pltpu.VMEM((tokens, width), BF16)

    rv, logits = call(
        logits_kernel,
        tallies,
        tuple(pltpu.with_memory_space_constraint(a, pltpu.HBM) for a in (flat, hq, hk, hv)),
        [pltpu.HBM] * 4,
        [(tokens, width), (H * positions, positions)],
        [block, square, square, square, block, block, block, pltpu.SemaphoreType.DMA((4,))],
        6 * tokens * width * width,
        "row_logits",
    )
    parts = exchange(logits.reshape(groups, share, positions))
    (copies,) = call(
        weights_kernel,
        tallies,
        (parts,),
        [pltpu.VMEM],
        [(groups, share, positions)],
        [],
        1 << 20,
        "row_weights",
    )
    weights = exchange(copies).reshape(H * positions, positions)
    row_out, send = call(
        mix_kernel,
        tallies,
        (weights, rv, flat),
        [pltpu.VMEM] * 3,
        [(tokens, width)] * 2,
        [pltpu.VMEM((sequences, positions, width), F32)],
        4 * tokens * width * positions,
        "row_mix",
    )
    columns = positions // groups
    lanes = 2 * LANES
    got = exchange(send.reshape(groups, tokens // groups, width)).reshape(tokens, width)
    (out,) = call(
        column_kernel,
        tallies,
        (got, vq, vk, vv),
        [pltpu.VMEM] * 4,
        [(groups, columns // 2, 16, width)],
        [pltpu.VMEM((width // lanes, columns, tokens // columns, lanes), BF16)] * 3,
        6 * tokens * width * width,
        "columns",
    )
    back = exchange(out.reshape(groups, tokens // groups, width))
    result = jnp.swapaxes(back.reshape(positions, sequences, width), 0, 1)
    return row_out.reshape(sequences, positions, width), result


def solution(mesh):
    whole = P(("aln", "seq"), None, None)
    in_specs = (whole, P("aln"), P(), P(), P(), P(), P(), P())
    return jax.shard_map(
        local, mesh=mesh, in_specs=in_specs, out_specs=(whole, whole), check_vma=False
    )
```

```python
import math

import jax
import jax.numpy as jnp
from jax import lax
from jax.experimental import pallas as pl
from jax.experimental.pallas import tpu as pltpu
from jax.sharding import PartitionSpec as P

H = 12
DH = 64
SEQ = "seq"
LANES = 128
EPS = 1e-05
BF16 = jnp.bfloat16
F32 = jnp.float32
NT = (((1,), (1,)), ((), ()))


def standardize(values):
    centre = jnp.mean(values, axis=-1, keepdims=True)
    shifted = values - centre
    spread = jnp.mean(shifted * shifted, axis=-1, keepdims=True)
    return shifted * lax.rsqrt(spread + EPS)


def half_masks():
    lane = lax.broadcasted_iota(jnp.int32, (1, LANES), 1)
    low = (lane < DH).astype(F32)
    return low.astype(BF16), (1.0 - low).astype(BF16)


def lane_block(value, index):
    return value[:, index * LANES : (index + 1) * LANES]


def hold_second_core(duration):
    @pl.when(lax.rem(lax.axis_index("aln"), 2) == 1)
    def _():
        pl.delay(duration)


def fetch(refs, sems):
    copies = [pltpu.make_async_copy(src, dst, sems.at[i]) for i, (src, dst) in enumerate(refs)]
    for copy in copies:
        copy.start()
    return copies


def logits_kernel(
    tally, x_hbm, wq_hbm, wk_hbm, wv_hbm, rv_ref, logits_ref, x_ref, wq_ref, wk_ref, wv_ref, n_ref, q_ref, k_ref, sems
):
    hold_second_core(FIRST_STAGGER)
    tokens = x_ref.shape[0]
    positions = logits_ref.shape[1]
    sequences = tokens // positions
    first, count = lax.axis_index(SEQ) * sequences, tally[0]
    early, late = pl.ds(0, tokens // 2), pl.ds(tokens // 2, tokens // 2)
    copies = fetch(
        (
            (x_hbm.at[early], x_ref.at[early]),
            (wq_hbm, wq_ref),
            (x_hbm.at[late], x_ref.at[late]),
            (wk_hbm, wk_ref),
            (wv_hbm, wv_ref),
        ),
        sems,
    )
    size = 2 * positions
    blocks = [slice(start, start + size) for start in range(0, tokens, size)]

    def norm(part):
        n_ref[part, :] = standardize(x_ref[part, :].astype(F32)).astype(BF16)

    def query(part):
        q = jnp.dot(n_ref[part, :], wq_ref[...], preferred_element_type=F32)
        for s in range(2):
            at = part.start + s * positions
            live = (first + at // positions < count).astype(F32)
            q_ref[at : at + positions, :] = (q[s * positions : (s + 1) * positions] * live).astype(BF16)

    def plain(part, source, target):
        target[part, :] = jnp.dot(n_ref[part, :], source[...], preferred_element_type=F32).astype(BF16)

    half = len(blocks) // 2
    copies[0].wait()
    for part in blocks[:half]:
        norm(part)
    copies[1].wait()
    copies[2].wait()
    for at, part in enumerate(blocks):
        query(part)
        if at < half:
            norm(blocks[half + at])
    copies[3].wait()
    copies[4].wait()
    for part in blocks:
        plain(part, wk_ref, k_ref)
    for part in blocks:
        plain(part, wv_ref, rv_ref)
    low, high = half_masks()
    for pair in range(H // 2):
        lanes = slice(pair * LANES, (pair + 1) * LANES)
        got = None
        for s in range(0, sequences, 2):
            rows = [slice((s + e) * positions, (s + e + 1) * positions) for e in range(2)]
            queries = [q_ref[r, lanes] for r in rows]
            even = jnp.concatenate([q * low for q in queries], axis=1)
            odd = jnp.concatenate([q * high for q in queries], axis=1)
            keys = jnp.concatenate([k_ref[r, lanes] for r in rows], axis=1)
            term = lax.dot_general(
                jnp.concatenate([even, odd], axis=0), keys, NT, preferred_element_type=F32
            )
            got = term if got is None else got + term
        at = 2 * pair * positions
        logits_ref[at : at + 2 * positions, :] = got.astype(BF16)


def weights_kernel(tally, parts_ref, out_ref):
    logits = parts_ref[0].astype(F32)
    for source in range(1, parts_ref.shape[0]):
        logits += parts_ref[source].astype(F32)
    count = jnp.full((1, 1), tally[0], jnp.int32).astype(F32)
    logits = logits / (jnp.sqrt(F32(DH)) * jnp.sqrt(count))
    top = jnp.max(logits, axis=-1, keepdims=True)
    powers = jnp.exp(logits - top)
    weights = (powers / jnp.sum(powers, axis=-1, keepdims=True)).astype(BF16)
    for target in range(out_ref.shape[0]):
        out_ref[target] = weights


def mix_kernel(tally, w_ref, rv_ref, x_ref, row_ref, send_ref, held):
    hold_second_core(SECOND_STAGGER)
    sequences, positions, width = held.shape
    first, count = lax.axis_index(SEQ) * sequences, tally[0]
    low, high = half_masks()
    for start in range(0, sequences, 2):
        mixed = [[], []]
        for pair in range(H // 2):
            at = 2 * pair * positions
            weights = jnp.concatenate(
                [w_ref[at : at + positions, :], w_ref[at + positions : at + 2 * positions, :]], axis=1
            )
            lanes = slice(pair * LANES, (pair + 1) * LANES)
            values = []
            for s in range(2):
                v = rv_ref[(start + s) * positions : (start + s + 1) * positions, lanes]
                values.append(jnp.concatenate([v * low, v * high], axis=0))
            got = jnp.dot(weights, jnp.concatenate(values, axis=1), preferred_element_type=F32)
            for s in range(2):
                mixed[s].append(lane_block(got, s))
        for s in range(2):
            live = (first + start + s < count).astype(F32)
            part = slice((start + s) * positions, (start + s + 1) * positions)
            out = (jnp.concatenate(mixed[s], axis=1) * live).astype(BF16)
            row_ref[part, :] = out
            held[start + s] = standardize(x_ref[part, :].astype(F32) + out.astype(F32))
    size = 16
    span = size * sequences
    for block in range(positions // size):
        turned = jnp.swapaxes(held[:, block * size : (block + 1) * size, :], 0, 1)
        send_ref[block * span : (block + 1) * span, :] = turned.reshape(span, width).astype(BF16)


def column_kernel(tally, n_ref, wq_ref, wk_ref, wv_ref, out_ref, q_ref, k_ref, v_ref):
    rows, width = n_ref.shape
    sets, columns, total, lanes = q_ref.shape
    factor = math.log2(math.e) / math.sqrt(DH)
    low, high = half_masks()
    lane = lax.broadcasted_iota(jnp.int32, (1, LANES), 1)
    is_low = lane < DH
    one_high = (lane == DH).astype(F32).astype(BF16)
    one_low = (lane == 0).astype(F32).astype(BF16)
    alive = lax.broadcasted_iota(jnp.int32, (total, 1), 0) < tally[0]
    bias = jnp.where(alive, 0.0, -1e30).astype(F32)
    bias_high = jnp.where(is_low, 0.0, bias).astype(BF16)
    bias_low = jnp.where(is_low, bias, 0.0).astype(BF16)
    live = alive.astype(F32)
    size = 256
    each = size // (8 * columns)

    def project(part, start, source, target, scale):
        got = jnp.dot(
            n_ref[start : start + size, :],
            source[:, part * lanes : (part + 1) * lanes],
            preferred_element_type=F32,
        )
        if scale is not None:
            got = got * scale
        got = got.reshape(each, columns, 8, lanes)
        at = start // columns
        for c in range(columns):
            target[part, c, at : at + each * 8, :] = got[:, c].reshape(each * 8, lanes).astype(BF16)

    def mix(q, k, v):
        scores = lax.dot_general(q, k, NT, preferred_element_type=F32)
        powers = jnp.exp2(scores - jnp.max(scores, axis=-1, keepdims=True)).astype(BF16)
        return jnp.dot(powers, v, preferred_element_type=F32)

    def attend(part, first, pair):
        outs = []
        span = slice(pair * LANES, (pair + 1) * LANES)
        for c in (first, first + 1):
            q, k, v = q_ref[part, c, :, span], k_ref[part, c, :, span], v_ref[part, c, :, span]
            even = mix(q * low + one_high, k * low + bias_high, v * low + high)
            odd = mix(q * high + one_low, k * high + bias_low, v * high + low)
            values = jnp.where(is_low, even, odd)
            sums = jnp.where(is_low, odd, even)
            outs.append((values * (live / pltpu.roll(sums, DH, 1))).reshape(total // 8, 8, LANES))
        at = part * lanes + pair * LANES
        both = jnp.stack(outs, axis=1).reshape(total // 8, 16, LANES)
        out_ref[:, first // 2, :, at : at + LANES] = both.astype(BF16)

    for part in range(sets):
        for start in range(0, rows, size):
            project(part, start, wq_ref, q_ref, factor)
            project(part, start, wk_ref, k_ref, None)
            project(part, start, wv_ref, v_ref, None)
        for first in range(0, columns, 2):
            for pair in range(lanes // LANES):
                attend(part, first, pair)


def call(kernel, tally, args, spaces, shapes, scratch, flops, name):
    specs = [pl.BlockSpec(memory_space=pltpu.SMEM)]
    return pl.pallas_call(
        kernel,
        in_specs=specs + [pl.BlockSpec(memory_space=s) for s in spaces],
        out_specs=[pl.BlockSpec(memory_space=pltpu.VMEM)] * len(shapes),
        out_shape=[jax.ShapeDtypeStruct(s, BF16) for s in shapes],
        scratch_shapes=scratch,
        cost_estimate=pl.CostEstimate(flops=flops, bytes_accessed=6 << 20, transcendentals=0),
        compiler_params=pltpu.CompilerParams(vmem_limit_bytes=24 << 20),
        name=name,
    )(tally, *args)


FIRST_STAGGER = 10500
SECOND_STAGGER = 11500


def exchange(value):
    return lax.all_to_all(value, SEQ, split_axis=0, concat_axis=0, tiled=True)


def local(x, tallies, hq, hk, hv, vq, vk, vv):
    sequences, positions, width = x.shape
    groups = lax.axis_size(SEQ)
    tokens = sequences * positions
    flat = x.reshape(tokens, width)
    share = H * positions // groups
    square = pltpu.VMEM((width, width), BF16)
    block = pltpu.VMEM((tokens, width), BF16)

    rv, logits = call(
        logits_kernel,
        tallies,
        tuple(pltpu.with_memory_space_constraint(a, pltpu.HBM) for a in (flat, hq, hk, hv)),
        [pltpu.HBM] * 4,
        [(tokens, width), (H * positions, positions)],
        [block, square, square, square, block, block, block, pltpu.SemaphoreType.DMA((5,))],
        6 * tokens * width * width,
        "row_logits",
    )
    parts = exchange(logits.reshape(groups, share, positions))
    (copies,) = call(
        weights_kernel,
        tallies,
        (parts,),
        [pltpu.VMEM],
        [(groups, share, positions)],
        [],
        1 << 20,
        "row_weights",
    )
    weights = exchange(copies).reshape(H * positions, positions)
    row_out, send = call(
        mix_kernel,
        tallies,
        (weights, rv, flat),
        [pltpu.VMEM] * 3,
        [(tokens, width)] * 2,
        [pltpu.VMEM((sequences, positions, width), F32)],
        4 * tokens * width * positions,
        "row_mix",
    )
    columns = positions // groups
    lanes = 2 * LANES
    got = exchange(send.reshape(groups, tokens // groups, width)).reshape(tokens, width)
    (out,) = call(
        column_kernel,
        tallies,
        (got, vq, vk, vv),
        [pltpu.VMEM] * 4,
        [(groups, columns // 2, 16, width)],
        [pltpu.VMEM((width // lanes, columns, tokens // columns, lanes), BF16)] * 3,
        6 * tokens * width * width,
        "columns",
    )
    back = exchange(out.reshape(groups, tokens // groups, width))
    result = jnp.swapaxes(back.reshape(positions, sequences, width), 0, 1)
    return row_out.reshape(sequences, positions, width), result


def solution(mesh):
    whole = P(("aln", "seq"), None, None)
    in_specs = (whole, P("aln"), P(), P(), P(), P(), P(), P())
    return jax.shard_map(
        local, mesh=mesh, in_specs=in_specs, out_specs=(whole, whole), check_vma=False
    )
```

```python
import math

import jax
import jax.numpy as jnp
from jax import lax
from jax.experimental import pallas as pl
from jax.experimental.pallas import tpu as pltpu
from jax.sharding import PartitionSpec as P

H = 12
DH = 64
SEQ = "seq"
LANES = 128
EPS = 1e-05
BF16 = jnp.bfloat16
F32 = jnp.float32
NT = (((1,), (1,)), ((), ()))


def standardize(values):
    centre = jnp.mean(values, axis=-1, keepdims=True)
    shifted = values - centre
    spread = jnp.mean(shifted * shifted, axis=-1, keepdims=True)
    return shifted * lax.rsqrt(spread + EPS)


def half_masks():
    lane = lax.broadcasted_iota(jnp.int32, (1, LANES), 1)
    low = (lane < DH).astype(F32)
    return low.astype(BF16), (1.0 - low).astype(BF16)


def lane_block(value, index):
    return value[:, index * LANES : (index + 1) * LANES]


def hold_second_core(duration):
    @pl.when(lax.rem(lax.axis_index("aln"), 2) == 1)
    def _():
        pl.delay(duration)


def fetch(refs, sems):
    copies = [pltpu.make_async_copy(src, dst, sems.at[i]) for i, (src, dst) in enumerate(refs)]
    for copy in copies:
        copy.start()
    return copies


def logits_kernel(
    tally, x_hbm, wq_hbm, wk_hbm, wv_hbm, rv_ref, logits_ref, x_ref, wq_ref, wk_ref, wv_ref, n_ref, q_ref, k_ref, sems
):
    hold_second_core(FIRST_STAGGER)
    tokens = x_ref.shape[0]
    positions = logits_ref.shape[1]
    sequences = tokens // positions
    first, count = lax.axis_index(SEQ) * sequences, tally[0]
    early, late = pl.ds(0, tokens // 2), pl.ds(tokens // 2, tokens // 2)
    copies = fetch(
        (
            (x_hbm.at[early], x_ref.at[early]),
            (wq_hbm, wq_ref),
            (x_hbm.at[late], x_ref.at[late]),
            (wk_hbm, wk_ref),
            (wv_hbm, wv_ref),
        ),
        sems,
    )
    size = 2 * positions
    blocks = [slice(start, start + size) for start in range(0, tokens, size)]

    def norm(part):
        n_ref[part, :] = standardize(x_ref[part, :].astype(F32)).astype(BF16)

    def query(part):
        q = jnp.dot(n_ref[part, :], wq_ref[...], preferred_element_type=F32)
        for s in range(2):
            at = part.start + s * positions
            live = (first + at // positions < count).astype(F32)
            q_ref[at : at + positions, :] = (q[s * positions : (s + 1) * positions] * live).astype(BF16)

    def plain(part, source, target):
        target[part, :] = jnp.dot(n_ref[part, :], source[...], preferred_element_type=F32).astype(BF16)

    half = len(blocks) // 2
    copies[0].wait()
    for part in blocks[:half]:
        norm(part)
    copies[1].wait()
    copies[2].wait()
    for at, part in enumerate(blocks):
        query(part)
        if at < half:
            norm(blocks[half + at])
    copies[3].wait()
    copies[4].wait()
    for part in blocks:
        plain(part, wk_ref, k_ref)
    for part in blocks:
        plain(part, wv_ref, rv_ref)
    low, high = half_masks()
    for pair in range(H // 2):
        lanes = slice(pair * LANES, (pair + 1) * LANES)
        got = None
        for s in range(0, sequences, 2):
            rows = [slice((s + e) * positions, (s + e + 1) * positions) for e in range(2)]
            queries = [q_ref[r, lanes] for r in rows]
            even = jnp.concatenate([q * low for q in queries], axis=1)
            odd = jnp.concatenate([q * high for q in queries], axis=1)
            keys = jnp.concatenate([k_ref[r, lanes] for r in rows], axis=1)
            term = lax.dot_general(
                jnp.concatenate([even, odd], axis=0), keys, NT, preferred_element_type=F32
            )
            got = term if got is None else got + term
        at = 2 * pair * positions
        logits_ref[at : at + 2 * positions, :] = got.astype(BF16)


def weights_kernel(tally, parts_ref, out_ref):
    logits = parts_ref[0].astype(F32)
    for source in range(1, parts_ref.shape[0]):
        logits += parts_ref[source].astype(F32)
    count = jnp.full((1, 1), tally[0], jnp.int32).astype(F32)
    logits = logits / (jnp.sqrt(F32(DH)) * jnp.sqrt(count))
    top = jnp.max(logits, axis=-1, keepdims=True)
    powers = jnp.exp(logits - top)
    weights = (powers / jnp.sum(powers, axis=-1, keepdims=True)).astype(BF16)
    for target in range(out_ref.shape[0]):
        out_ref[target] = weights


def mix_kernel(tally, w_ref, rv_ref, x_ref, row_ref, send_ref, held):
    hold_second_core(SECOND_STAGGER)
    sequences, positions, width = held.shape
    first, count = lax.axis_index(SEQ) * sequences, tally[0]
    low, high = half_masks()
    for start in range(0, sequences, 2):
        mixed = [[], []]
        for pair in range(H // 2):
            at = 2 * pair * positions
            weights = jnp.concatenate(
                [w_ref[at : at + positions, :], w_ref[at + positions : at + 2 * positions, :]], axis=1
            )
            lanes = slice(pair * LANES, (pair + 1) * LANES)
            values = []
            for s in range(2):
                v = rv_ref[(start + s) * positions : (start + s + 1) * positions, lanes]
                values.append(jnp.concatenate([v * low, v * high], axis=0))
            got = jnp.dot(weights, jnp.concatenate(values, axis=1), preferred_element_type=F32)
            for s in range(2):
                mixed[s].append(lane_block(got, s))
        for s in range(2):
            live = (first + start + s < count).astype(F32)
            part = slice((start + s) * positions, (start + s + 1) * positions)
            out = (jnp.concatenate(mixed[s], axis=1) * live).astype(BF16)
            row_ref[part, :] = out
            held[start + s] = standardize(x_ref[part, :].astype(F32) + out.astype(F32))
    size = 16
    span = size * sequences
    for block in range(positions // size):
        turned = jnp.swapaxes(held[:, block * size : (block + 1) * size, :], 0, 1)
        send_ref[block * span : (block + 1) * span, :] = turned.reshape(span, width).astype(BF16)


def column_kernel(tally, n_ref, wq_ref, wk_ref, wv_ref, out_ref, q_ref, k_ref, v_ref):
    rows, width = n_ref.shape
    sets, columns, total, lanes = q_ref.shape
    factor = math.log2(math.e) / math.sqrt(DH)
    low, high = half_masks()
    lane = lax.broadcasted_iota(jnp.int32, (1, LANES), 1)
    is_low = lane < DH
    one_high = (lane == DH).astype(F32).astype(BF16)
    one_low = (lane == 0).astype(F32).astype(BF16)
    alive = lax.broadcasted_iota(jnp.int32, (total, 1), 0) < tally[0]
    bias = jnp.where(alive, 0.0, -1e30).astype(F32)
    bias_high = jnp.where(is_low, 0.0, bias).astype(BF16)
    bias_low = jnp.where(is_low, bias, 0.0).astype(BF16)
    live = alive.astype(F32)
    size = 256
    each = size // (8 * columns)

    def project(part, start, source, target, scale):
        got = jnp.dot(
            n_ref[start : start + size, :],
            source[:, part * lanes : (part + 1) * lanes],
            preferred_element_type=F32,
        )
        if scale is not None:
            got = got * scale
        got = got.reshape(each, columns, 8, lanes)
        at = start // columns
        for c in range(columns):
            target[part, c, at : at + each * 8, :] = got[:, c].reshape(each * 8, lanes).astype(BF16)

    def mix(q, k, v):
        scores = lax.dot_general(q, k, NT, preferred_element_type=F32)
        powers = jnp.exp2(scores - jnp.max(scores, axis=-1, keepdims=True)).astype(BF16)
        return jnp.dot(powers, v, preferred_element_type=F32)

    def attend(part, first, pair):
        outs = []
        span = slice(pair * LANES, (pair + 1) * LANES)
        for c in (first, first + 1):
            q, k, v = q_ref[part, c, :, span], k_ref[part, c, :, span], v_ref[part, c, :, span]
            even = mix(q * low + one_high, k * low + bias_high, v * low + high)
            odd = mix(q * high + one_low, k * high + bias_low, v * high + low)
            values = jnp.where(is_low, even, odd)
            sums = jnp.where(is_low, odd, even)
            outs.append((values * (live / pltpu.roll(sums, DH, 1))).reshape(total // 8, 8, LANES))
        at = part * lanes + pair * LANES
        both = jnp.stack(outs, axis=1).reshape(total // 8, 16, LANES)
        out_ref[:, first // 2, :, at : at + LANES] = both.astype(BF16)

    for part in range(sets):
        for start in range(0, rows, size):
            project(part, start, wq_ref, q_ref, factor)
            project(part, start, wk_ref, k_ref, None)
            project(part, start, wv_ref, v_ref, None)
        for first in range(0, columns, 2):
            for pair in range(lanes // LANES):
                attend(part, first, pair)


def turn_kernel(recv_ref, out_hbm, held, sems):
    sequences, positions, width = held.shape
    size = 16
    copies = []
    for block in range(positions // size):
        part = pl.ds(block * size, size)
        got = recv_ref[block * size * sequences : (block + 1) * size * sequences, :].astype(F32)
        turned = jnp.swapaxes(got.reshape(size, sequences, width), 0, 1)
        held[:, block * size : (block + 1) * size, :] = turned.astype(BF16)
        copy = pltpu.make_async_copy(held.at[:, part, :], out_hbm.at[:, part, :], sems.at[block])
        copy.start()
        copies.append(copy)
    for copy in copies:
        copy.wait()


def call(kernel, tally, args, spaces, shapes, scratch, flops, name):
    specs = [pl.BlockSpec(memory_space=pltpu.SMEM)]
    return pl.pallas_call(
        kernel,
        in_specs=specs + [pl.BlockSpec(memory_space=s) for s in spaces],
        out_specs=[pl.BlockSpec(memory_space=pltpu.VMEM)] * len(shapes),
        out_shape=[jax.ShapeDtypeStruct(s, BF16) for s in shapes],
        scratch_shapes=scratch,
        cost_estimate=pl.CostEstimate(flops=flops, bytes_accessed=6 << 20, transcendentals=0),
        compiler_params=pltpu.CompilerParams(vmem_limit_bytes=24 << 20),
        name=name,
    )(tally, *args)


FIRST_STAGGER = 10500
SECOND_STAGGER = 11500


def exchange(value):
    return lax.all_to_all(value, SEQ, split_axis=0, concat_axis=0, tiled=True)


def local(x, tallies, hq, hk, hv, vq, vk, vv):
    sequences, positions, width = x.shape
    groups = lax.axis_size(SEQ)
    tokens = sequences * positions
    flat = x.reshape(tokens, width)
    share = H * positions // groups
    square = pltpu.VMEM((width, width), BF16)
    block = pltpu.VMEM((tokens, width), BF16)

    rv, logits = call(
        logits_kernel,
        tallies,
        tuple(pltpu.with_memory_space_constraint(a, pltpu.HBM) for a in (flat, hq, hk, hv)),
        [pltpu.HBM] * 4,
        [(tokens, width), (H * positions, positions)],
        [block, square, square, square, block, block, block, pltpu.SemaphoreType.DMA((5,))],
        6 * tokens * width * width,
        "row_logits",
    )
    parts = exchange(logits.reshape(groups, share, positions))
    (copies,) = call(
        weights_kernel,
        tallies,
        (parts,),
        [pltpu.VMEM],
        [(groups, share, positions)],
        [],
        1 << 20,
        "row_weights",
    )
    weights = exchange(copies).reshape(H * positions, positions)
    row_out, send = call(
        mix_kernel,
        tallies,
        (weights, rv, flat),
        [pltpu.VMEM] * 3,
        [(tokens, width)] * 2,
        [pltpu.VMEM((sequences, positions, width), F32)],
        4 * tokens * width * positions,
        "row_mix",
    )
    columns = positions // groups
    lanes = 2 * LANES
    got = exchange(send.reshape(groups, tokens // groups, width)).reshape(tokens, width)
    (out,) = call(
        column_kernel,
        tallies,
        (got, vq, vk, vv),
        [pltpu.VMEM] * 4,
        [(groups, columns // 2, 16, width)],
        [pltpu.VMEM((width // lanes, columns, tokens // columns, lanes), BF16)] * 3,
        6 * tokens * width * width,
        "columns",
    )
    back = exchange(out.reshape(groups, tokens // groups, width))
    result = pl.pallas_call(
        turn_kernel,
        in_specs=[pl.BlockSpec(memory_space=pltpu.VMEM)],
        out_specs=pl.BlockSpec(memory_space=pltpu.HBM),
        out_shape=jax.ShapeDtypeStruct((sequences, positions, width), BF16),
        scratch_shapes=[
            pltpu.VMEM((sequences, positions, width), BF16),
            pltpu.SemaphoreType.DMA((positions // 16,)),
        ],
        cost_estimate=pl.CostEstimate(flops=0, bytes_accessed=3 << 20, transcendentals=0),
        compiler_params=pltpu.CompilerParams(vmem_limit_bytes=24 << 20),
        name="turn_back",
    )(back.reshape(tokens, width))
    return row_out.reshape(sequences, positions, width), result


def solution(mesh):
    whole = P(("aln", "seq"), None, None)
    in_specs = (whole, P("aln"), P(), P(), P(), P(), P(), P())
    return jax.shard_map(
        local, mesh=mesh, in_specs=in_specs, out_specs=(whole, whole), check_vma=False
    )
```
